512 devices in a mesh: rows: 128 (over x, z, core), grp: 4 (over y).
Axes of the slice: x: 4, y: 4, z: 16, core: 2. Of those that a mesh axis runs over, the one named last changes fastest.
Arguments:
- a_blocks: float32 [4096, 7, 128, 128], P(('rows', 'grp')), may hold values from -0.5 to 0.5
- neighbours: int32 [4096, 7], P(('rows', 'grp')), may hold values from 0 to 4095, as said below
- neighbour_count: int32 [4096], P(('rows', 'grp')), may hold values from 1 to 7
- p_blocks: float32 [4096, 2, 128, 128], P(('rows', 'grp')), may hold values from -1 to 1
- p_columns: int32 [4096, 2], P(('rows', 'grp')), may hold values from 0 to 511, as said below
- p_count: int32 [4096], P(('rows', 'grp')), may hold values from 1 to 2
- coarse_slot: int32 [512], replicated, may hold values from 0 to 3, as said below
- coarse_pattern: int32 [512, 4], replicated, may hold values from 0 to 511, as said below
Outputs:
- coarse_op: float32 [512, 4, 128, 128], P(('rows', 'grp'))
The draws below stay inside these ranges and needn't reach their ends.
Inputs may be any that keep to these rules, and one draw needn't show every extreme that they name: neighbours[e,0] = e; every neighbour of an element of the slab of 32 elements that holds it lies in that slab or within 8 elements before or after it. The elements of slab q form aggregates q * 4 to (q + 1) * 4 - 1, eight elements each; p_columns[e,0] is the aggregate of e, and every slot names an aggregate of the element's slab or of a slab beside it. `coarse_slot`: within each slab the aggregates take each position 0 to 3 once. coarse_pattern[c,0] = c; every column is an aggregate of c's slab or of a slab beside it; columns may repeat.
All inputs are finite; a program needn't handle non-finite values.
Results may differ from the reference program's by a relative error of at most 0.0003.
Values sent between devices are 32-bit elements; how exact they have to be, the bound alone decides.
A program may use at most 64 MiB of HBM per device.

```python
import jax
import jax.numpy as jnp
from jax import lax

B = 128
K = 7
KP = 2
KC = 4
SLAB = 32
AGG_SLAB = 4
RIM = 8
NE = 4096
NAGG = 512


def slab_permutation(key, count, length):
    scores = jax.random.randint(key, (count, length), 0, 1 << 20) * length + jnp.arange(length, dtype=jnp.int32)[None, :]
    return jnp.argsort(scores, axis=1).astype(jnp.int32)


def draw_neighbours(key, part):
    element = jnp.arange(NE, dtype=jnp.int32)
    slab_id = element // SLAB
    lower = jnp.maximum(slab_id * SLAB - RIM, 0)
    upper = jnp.minimum((slab_id + 1) * SLAB + RIM, NE)
    picks = jax.random.randint(key, (NE, K), lower[:, None], upper[:, None])
    return picks.at[:, 0].set(element).astype(jnp.int32)


def draw_neighbour_count(key, part):
    base = jax.random.randint(key, (NE,), 1, K + 1)
    index = jnp.arange(NE, dtype=jnp.int32)
    return jnp.where(index % 7 == 0, K, jnp.where(index % 7 == 1, 1, base)).astype(jnp.int32)


def draw_p_count(key, part):
    base = jax.random.randint(key, (NE,), 1, KP + 1)
    index = jnp.arange(NE, dtype=jnp.int32)
    return jnp.where(index % 5 == 0, KP, jnp.where(index % 5 == 1, 1, base)).astype(jnp.int32)


def draw_p_columns(key, part):
    slab_total = NE // SLAB
    order = slab_permutation(jax.random.fold_in(key, 11), slab_total, SLAB)
    slab_id = jnp.arange(NE, dtype=jnp.int32) // SLAB
    own = slab_id * AGG_SLAB + (order // 8).reshape(NE)
    lower = jnp.maximum(slab_id - 1, 0) * AGG_SLAB
    upper = jnp.minimum(slab_id + 2, slab_total) * AGG_SLAB
    others = jax.random.randint(jax.random.fold_in(key, 12), (NE, KP - 1), lower[:, None], upper[:, None])
    return jnp.concatenate([own[:, None], others], axis=1).astype(jnp.int32)


def draw_coarse_slot(key, part):
    order = slab_permutation(key, NAGG // AGG_SLAB, AGG_SLAB)
    return order.reshape(NAGG).astype(jnp.int32)


def draw_coarse_pattern(key, part):
    slab_total = NAGG // AGG_SLAB
    agg = jnp.arange(NAGG, dtype=jnp.int32)
    slab_id = agg // AGG_SLAB
    lower = jnp.maximum(slab_id - 1, 0) * AGG_SLAB
    upper = jnp.minimum(slab_id + 2, slab_total) * AGG_SLAB
    others = jax.random.randint(key, (NAGG, KC - 1), lower[:, None], upper[:, None])
    return jnp.concatenate([agg[:, None], others], axis=1).astype(jnp.int32)


def levels(stream_key, shape, split, low, high):
    loudness, own = 1.0, jax.random.fold_in(stream_key, 6)
    for axis_at, shards_of in split:
        draws = jnp.exp(jax.random.uniform(jax.random.fold_in(own, axis_at), (shards_of,), jnp.float32, low / len(split), high / len(split)))
        loudness = loudness * jnp.repeat(draws, shape[axis_at] // shards_of).reshape([-1 if axis == axis_at else 1 for axis in range(len(shape))])
    return loudness


def noise(stream_key, extent, spread, reach, shards=(), held_as=jnp.bfloat16):
    result = spread * jax.random.normal(stream_key, extent, jnp.float32)
    if shards:
        result = result * levels(stream_key, extent, shards, -0.22, 0.18)
    return jnp.clip(result, -reach, reach).astype(held_as)


def setup_inputs(seed: int = 0) -> dict:
    seeds = jax.random.split(jax.random.key(seed), 9)
    a_blocks = noise(seeds[0], (NE, K, B, B), B ** -0.5, 0.5, ((0, 512),), jnp.float32)
    neighbours = draw_neighbours(jax.random.fold_in(seeds[8], 71), 0)
    neighbour_count = draw_neighbour_count(jax.random.fold_in(seeds[8], 71), 0)
    p_blocks = noise(seeds[3], (NE, KP, B, B), 0.17, 1.0, ((0, 512),), jnp.float32)
    p_columns = draw_p_columns(jax.random.fold_in(seeds[8], 71), 0)
    p_count = draw_p_count(jax.random.fold_in(seeds[8], 71), 0)
    coarse_slot = draw_coarse_slot(jax.random.fold_in(seeds[8], 71), 0)
    coarse_pattern = draw_coarse_pattern(jax.random.fold_in(seeds[8], 71), 0)
    return dict(a_blocks=a_blocks, neighbours=neighbours, neighbour_count=neighbour_count, p_blocks=p_blocks, p_columns=p_columns, p_count=p_count, coarse_slot=coarse_slot, coarse_pattern=coarse_pattern)


HIGH = lax.Precision.HIGHEST


def reference(a_blocks, neighbours, neighbour_count, p_blocks, p_columns, p_count, coarse_slot, coarse_pattern):
    slab_count = NE // SLAB

    def one_slab(galerkin, slab_id):
        start = (slab_id * SLAB).astype(jnp.int32)
        blocks = lax.dynamic_slice_in_dim(a_blocks, start, SLAB, 0)
        near = lax.dynamic_slice_in_dim(neighbours, start, SLAB, 0)
        near_count = lax.dynamic_slice_in_dim(neighbour_count, start, SLAB, 0)
        own_p = lax.dynamic_slice_in_dim(p_blocks, start, SLAB, 0)
        own_cols = lax.dynamic_slice_in_dim(p_columns, start, SLAB, 0)
        own_count = lax.dynamic_slice_in_dim(p_count, start, SLAB, 0)
        near_p = jnp.take(p_blocks, near, axis=0)
        near_cols = jnp.take(p_columns, near, axis=0)
        near_live = jnp.arange(KP, dtype=jnp.int32)[None, None, :] < jnp.take(p_count, near, axis=0)[:, :, None]
        slot_live = jnp.arange(K, dtype=jnp.int32)[None, :] < near_count[:, None]
        own_live = jnp.arange(KP, dtype=jnp.int32)[None, :] < own_count[:, None]
        products = jnp.einsum('ekab,ekjbc->ekjac', blocks, near_p, precision=HIGH)
        targets = jnp.take(coarse_pattern, own_cols, axis=0)
        select = (slot_live[:, None, None, :, None] & own_live[:, :, None, None, None]
                  & near_live[:, None, None, :, :]
                  & (near_cols[:, None, None, :, :] == targets[:, :, :, None, None])).astype(jnp.float32)
        summed = jnp.einsum('ejskl,eklac->ejsac', select, products, precision=HIGH)
        terms = jnp.einsum('ejba,ejsbc->ejsac', own_p, summed, precision=HIGH)
        galerkin = galerkin.at[own_cols.reshape(-1)].add(terms.reshape(SLAB * KP, KC, B, B))
        return galerkin, None

    start_value = jnp.zeros((NAGG, KC, B, B), jnp.float32)
    galerkin, unused = lax.scan(one_slab, start_value, jnp.arange(slab_count, dtype=jnp.int32))
    places = (jnp.arange(NAGG, dtype=jnp.int32) // AGG_SLAB) * AGG_SLAB + coarse_slot
    return jnp.zeros((NAGG, KC, B, B), jnp.float32).at[places].set(galerkin)
```

```python
import functools

import jax
import jax.numpy as jnp
from jax import lax
from jax.experimental import pallas as pl
from jax.experimental.pallas import tpu as pltpu
from jax.sharding import PartitionSpec as P

MESH = pl.DeviceIdType.MESH
F32, BF16, I32 = jnp.float32, jnp.bfloat16, jnp.int32
ORDER = ((2, 0), (2, 1), (1, 1), (3, 0), (1, 0), (3, 1), (0, 0), (0, 1))


def split(value):
    high = value.astype(BF16)
    return high, (value - high.astype(F32)).astype(BF16)


def kernel(
    n_rows, a_hbm, near, near_count, p_hbm, cols, count, slot, pattern, out,
    a_f32, a3, p_win, p3, pt3, prod, z3, terms, meta, meta_s,
    to_prev, to_next, from_next, from_prev, own, from_y,
    a_sem, p_sem, m_sem,
    yp_s, yp_r, ym_s, ym_r, zp_s, zp_r, zm_s, zm_r,
    tn_s, tn_r, tp_s, tp_r, ty_s, ty_r,
):
    e_local, n_slot, size = a_hbm.shape[0], a_hbm.shape[1], a_hbm.shape[2]
    half = e_local // 2
    q, g = lax.axis_index("rows"), lax.axis_index("grp")
    up, down, opp = lax.rem(g + 1, 4), lax.rem(g + 3, 4), lax.rem(g + 2, 4)
    has_prev, has_next = q > 0, q < n_rows - 1
    yp, ym = {"grp": up}, {"grp": down}
    zp, zm = {"rows": q + 1}, {"rows": q - 1}

    def copy(src, dst, ssem, rsem, dev):
        return pltpu.make_async_remote_copy(
            src_ref=src, dst_ref=dst, send_sem=ssem, recv_sem=rsem,
            device_id=dev, device_id_type=MESH,
        )

    own_copy = pltpu.make_async_copy(
        p_hbm, p_win.at[pl.ds(e_local + e_local * g, e_local)], p_sem.at[0]
    )
    own_copy.start()
    a_copies = [
        pltpu.make_async_copy(a_hbm.at[e], a_f32.at[e], a_sem.at[e])
        for e in range(e_local)
    ]
    for c in a_copies:
        c.start()

    row_id = lax.broadcasted_iota(I32, (8, 128), 0)
    lane_id = lax.broadcasted_iota(I32, (8, 128), 1)
    tile = jnp.zeros((8, 128), I32)
    for e in range(e_local):
        for lane, value in ((0, cols[0, e]), (1, cols[1, e]), (2, count[e])):
            tile = jnp.where((row_id == e) & (lane_id == lane), value, tile)
    meta[1 + g] = tile

    @pl.when(q == 0)
    def _():
        meta[0] = jnp.zeros((8, 128), I32)
        for i in range(8):
            from_prev[i] = jnp.zeros(from_prev.shape[1:], F32)

    @pl.when(q == n_rows - 1)
    def _():
        meta[5] = jnp.zeros((8, 128), I32)
        for i in range(8):
            from_next[i] = jnp.zeros(from_next.shape[1:], F32)

    barrier = pltpu.get_barrier_semaphore()
    for dev in (yp, ym):
        pl.semaphore_signal(barrier, inc=1, device_id=dev, device_id_type=MESH)

    @pl.when(has_next)
    def _():
        pl.semaphore_signal(barrier, inc=1, device_id=zp, device_id_type=MESH)

    @pl.when(has_prev)
    def _():
        pl.semaphore_signal(barrier, inc=1, device_id=zm, device_id_type=MESH)

    pl.semaphore_wait(barrier, 2 + has_next.astype(I32) + has_prev.astype(I32))

    def place(src_g, e):
        return p_win.at[e_local + e_local * src_g + e]

    def send_yp(i):
        if i < 8:
            src, dst = p_hbm.at[i], place(g, i)
        elif i == 8:
            src = dst = meta.at[1 + g]
        elif i < 13:
            src = dst = place(down, i - 9)
        else:
            src = dst = meta.at[1 + down]
        return copy(src, dst, yp_s.at[i], yp_r.at[i], yp)

    def send_ym(i):
        if i < 8:
            src, dst = p_hbm.at[i], place(g, i)
        elif i == 8:
            src = dst = meta.at[1 + g]
        else:
            src = dst = place(up, half + i - 9)
        return copy(src, dst, ym_s.at[i], ym_r.at[i], ym)

    def send_zp(e):
        if e < 8:
            src, dst = place(3, e), p_win.at[e]
        else:
            src, dst = meta.at[4], meta.at[0]
        return copy(src, dst, zp_s.at[e], zp_r.at[e], zp)

    def send_zm(e):
        if e < 8:
            src, dst = place(0, e), p_win.at[5 * e_local + e]
        else:
            src, dst = meta.at[1], meta.at[5]
        return copy(src, dst, zm_s.at[e], zm_r.at[e], zm)

    def rim(src_g, e):
        @pl.when((src_g == 3) & has_next)
        def _():
            send_zp(e).start()

        @pl.when((src_g == 0) & has_prev)
        def _():
            send_zm(e).start()

    def widen(index):
        for l in range(2):
            high, low = split(p_win[index, l])
            lanes = pl.ds(l * size, size)
            p3[index, pl.ds(0, size), lanes] = high
            p3[index, pl.ds(size, size), lanes] = high
            p3[index, pl.ds(2 * size, size), lanes] = low

    def prepare(e):
        a_copies[e].wait()
        for k in range(n_slot):
            high, low = split(a_f32[e, k])
            a3[e * n_slot + k, :, pl.ds(0, size)] = high
            a3[e * n_slot + k, :, pl.ds(size, size)] = low
            a3[e * n_slot + k, :, pl.ds(2 * size, size)] = high
        for j in range(2):
            high, low = split(p_win[e_local + e_local * g + e, j].T)
            pt3[2 * e + j, :, pl.ds(0, size)] = high
            pt3[2 * e + j, :, pl.ds(size, size)] = low
            pt3[2 * e + j, :, pl.ds(2 * size, size)] = high

    send_yp(8).start()
    send_ym(8).start()
    for i in range(half):
        send_yp(i).start()
        send_ym(half + i).start()
    own_copy.wait()
    for e in range(9):
        rim(g, e)
    send_yp(8).wait_recv()
    send_yp(13).start()
    rim(down, 8)
    send_ym(8).wait_recv()
    rim(up, 8)
    for e in range(e_local):
        widen(e_local + e_local * g + e)
    for i in range(half):
        send_yp(i).wait_recv()
        send_yp(9 + i).start()
        send_yp(half + i).start()
        rim(down, i)
        send_ym(half + i).wait_recv()
        send_ym(9 + i).start()
        send_ym(i).start()
        rim(up, half + i)
        if i == 0:
            send_yp(13).wait_recv()
            rim(opp, 8)
        widen(e_local + e_local * down + i)
        widen(e_local + e_local * up + half + i)
        prepare(2 * i)
        prepare(2 * i + 1)
    for i in range(half):
        send_yp(9 + i).wait_recv()
        rim(opp, i)
        send_ym(9 + i).wait_recv()
        rim(opp, half + i)
        send_yp(half + i).wait_recv()
        rim(down, half + i)
        send_ym(i).wait_recv()
        rim(up, i)
        widen(e_local + e_local * opp + i)
        widen(e_local + e_local * opp + half + i)
        widen(e_local + e_local * down + half + i)
        widen(e_local + e_local * up + i)

    @pl.when(has_prev)
    def _():
        send_zp(8).wait_recv()

    @pl.when(has_next)
    def _():
        send_zm(8).wait_recv()

    meta_copy = pltpu.make_async_copy(meta, meta_s, m_sem.at[0])
    meta_copy.start()
    for e in range(e_local):
        @pl.when(has_prev)
        def _():
            send_zp(e).wait_recv()
            widen(e)

        @pl.when(has_next)
        def _():
            send_zm(e).wait_recv()
            widen(5 * e_local + e)
    meta_copy.wait()

    base = q * (4 * e_local) - e_local

    def element(e, carry):
        columns = []
        live_k = near_count[e]
        for k in range(n_slot):
            n = jnp.clip(near[e, k] - base, 0, 6 * e_local - 1)
            n_hi, n_lo = lax.shift_right_logical(n, 3), n & 7
            live_l = jnp.where(k < live_k, meta_s[n_hi, n_lo, 2], 0)
            for l in range(2):
                columns.append(jnp.where(l < live_l, meta_s[n_hi, n_lo, l], -1))
            prod[k] = jnp.dot(
                a3[e * n_slot + k], p3[n], preferred_element_type=F32
            )
        live_j = count[e]
        for j in range(2):
            c = cols[j, e]
            for s in range(4):
                target = jnp.where(j < live_j, pattern[s, c], -2)
                total = None
                for k in range(n_slot):
                    for l in range(2):
                        match = jnp.where(columns[2 * k + l] == target, 1.0, 0.0)
                        part = prod[k, :, pl.ds(l * size, size)] * match
                        total = part if total is None else total + part
                high, low = split(total)
                lanes = pl.ds(s * size, size)
                z3[j, pl.ds(0, size), lanes] = high
                z3[j, pl.ds(size, size), lanes] = high
                z3[j, pl.ds(2 * size, size), lanes] = low
            term = jnp.dot(pt3[2 * e + j], z3[j], preferred_element_type=F32)
            for s in range(4):
                terms[2 * e + j, s] = term[:, s * size : (s + 1) * size]
        return carry

    lax.fori_loop(0, e_local, element, 0)

    where = []
    for e in range(e_local):
        for j in range(2):
            c = cols[j, e]
            where.append((lax.shift_right_logical(c, 2) - q + 1) * 4 + slot[c])

    def gather_rows(dst, i, first, slots):
        rel, h = ORDER[i]
        target = first + lax.rem(g + rel, 4)
        for s in range(2):
            total = None
            for x in slots:
                match = jnp.where(where[x] == target, 1.0, 0.0)
                part = terms[x, 2 * h + s] * match
                total = part if total is None else total + part
            dst[i, s] = total

    def send_tp(i):
        return copy(to_prev.at[i], from_next.at[i], tp_s.at[i], tp_r.at[i], zm)

    def send_tn(i):
        return copy(to_next.at[i], from_prev.at[i], tn_s.at[i], tn_r.at[i], zp)

    seconds = [2 * e + 1 for e in range(e_local)]
    for i in range(8):
        @pl.when(has_prev)
        def _():
            gather_rows(to_prev, i, 0, seconds)
            send_tp(i).start()

        @pl.when(has_next)
        def _():
            gather_rows(to_next, i, 8, seconds)
            send_tn(i).start()

    for i in range(8):
        gather_rows(own, i, 4, range(2 * e_local))

    def send_y(i):
        return copy(
            own.at[i], from_y.at[i], ty_s.at[i], ty_r.at[i], yp if i in (0, 2, 4) else ym
        )

    for i in range(8):
        @pl.when(has_next)
        def _():
            send_tp(i).wait_recv()

        @pl.when(has_prev)
        def _():
            send_tn(i).wait_recv()

        total = own[i] + (from_next[i] + from_prev[i])
        if i in (4, 5):
            send_y(i - 4).wait_recv()
            total = total + from_y[i - 4]
        own[i] = total
        if i < 6:
            send_y(i).start()
    for i in (3, 2, 4, 5):
        send_y(i).wait_recv()
    for s in range(2):
        out[0, s] = own[6, s] + (from_y[4, s] + from_y[3, s])
        out[0, 2 + s] = own[7, s] + (from_y[2, s] + from_y[5, s])

    for i in range(14):
        send_yp(i).wait_send()
    for i in range(13):
        send_ym(i).wait_send()

    @pl.when(has_next)
    def _():
        for e in range(9):
            send_zp(e).wait_send()
        for i in range(8):
            send_tn(i).wait_send()

    @pl.when(has_prev)
    def _():
        for e in range(9):
            send_zm(e).wait_send()
        for i in range(8):
            send_tp(i).wait_send()

    for i in range(6):
        send_y(i).wait_send()


def per_device(a, near, near_count, p, cols, count, slot, pattern):
    e_local, n_slot, size = a.shape[0], a.shape[1], a.shape[2]
    smem = pl.BlockSpec(memory_space=pltpu.SMEM)
    anywhere = pl.BlockSpec(memory_space=pl.ANY)
    dma = pltpu.SemaphoreType.DMA
    block = (size, size)
    return pl.pallas_call(
        functools.partial(kernel, lax.axis_size("rows")),
        out_shape=jax.ShapeDtypeStruct((1, 4) + block, F32),
        in_specs=[anywhere, smem, smem, anywhere, smem, smem, smem, smem],
        out_specs=pl.BlockSpec(memory_space=pltpu.VMEM),
        scratch_shapes=[
            pltpu.VMEM(a.shape, F32),
            pltpu.VMEM((e_local * n_slot, size, 3 * size), BF16),
            pltpu.VMEM((6 * e_local, 2) + block, F32),
            pltpu.VMEM((6 * e_local, 3 * size, 2 * size), BF16),
            pltpu.VMEM((2 * e_local, size, 3 * size), BF16),
            pltpu.VMEM((n_slot, size, 2 * size), F32),
            pltpu.VMEM((2, 3 * size, 4 * size), BF16),
            pltpu.VMEM((2 * e_local, 4) + block, F32),
            pltpu.VMEM((6, 8, 128), I32),
            pltpu.SMEM((6, 8, 128), I32),
        ]
        + [pltpu.VMEM((8, 2) + block, F32)] * 5
        + [pltpu.VMEM((6, 2) + block, F32)]
        + [dma((e_local,)), dma((1,)), dma((1,))]
        + [dma((14,)), dma((14,)), dma((13,)), dma((13,))]
        + [dma((9,))] * 4
        + [dma((8,))] * 4
        + [dma((6,))] * 2,
        compiler_params=pltpu.CompilerParams(
            collective_id=0, has_side_effects=True, vmem_limit_bytes=56 << 20
        ),
    )(a, near, near_count, p, cols.T, count, slot, pattern.T)


def solution(mesh):
    return jax.shard_map(
        per_device,
        mesh=mesh,
        in_specs=(
            P(("rows", "grp"), None, None, None),
            P(("rows", "grp"), None),
            P(("rows", "grp")),
            P(("rows", "grp"), None, None, None),
            P(("rows", "grp"), None),
            P(("rows", "grp")),
            P(),
            P(),
        ),
        out_specs=P(("rows", "grp"), None, None, None),
        check_vma=False,
    )
```

```python
import functools

import jax
import jax.numpy as jnp
from jax import lax
from jax.experimental import pallas as pl
from jax.experimental.pallas import tpu as pltpu
from jax.sharding import PartitionSpec as P

MESH = pl.DeviceIdType.MESH
F32, BF16, I32 = jnp.float32, jnp.bfloat16, jnp.int32
ORDER = ((2, 0), (2, 1), (1, 1), (3, 0), (1, 0), (3, 1), (0, 0), (0, 1))


def split(value):
    high = value.astype(BF16)
    return high, (value - high.astype(F32)).astype(BF16)


def kernel(
    n_rows, a_hbm, near, near_count, p_hbm, cols, count, slot, pattern, out,
    a_f32, a3, p_win, p3, pt3, sums_a, sums_b, z_a, z_b, terms, meta, meta_s,
    n_s, prev_s, last_s,
    to_prev, to_next, from_next, from_prev, own, from_y,
    a_sem, p_sem, m_sem,
    yp_s, yp_r, ym_s, ym_r, zp_s, zp_r, zm_s, zm_r,
    tn_s, tn_r, tp_s, tp_r, ty_s, ty_r,
):
    e_local, n_slot, size = a_hbm.shape[0], a_hbm.shape[1], a_hbm.shape[2]
    half = e_local // 2
    q, g = lax.axis_index("rows"), lax.axis_index("grp")
    up, down, opp = lax.rem(g + 1, 4), lax.rem(g + 3, 4), lax.rem(g + 2, 4)
    has_prev, has_next = q > 0, q < n_rows - 1
    yp, ym = {"grp": up}, {"grp": down}
    zp, zm = {"rows": q + 1}, {"rows": q - 1}

    def copy(src, dst, ssem, rsem, dev):
        return pltpu.make_async_remote_copy(
            src_ref=src, dst_ref=dst, send_sem=ssem, recv_sem=rsem,
            device_id=dev, device_id_type=MESH,
        )

    own_copy = pltpu.make_async_copy(
        p_hbm, p_win.at[pl.ds(e_local + e_local * g, e_local)], p_sem.at[0]
    )
    own_copy.start()
    a_copies = [
        pltpu.make_async_copy(a_hbm.at[e], a_f32.at[e], a_sem.at[e])
        for e in range(e_local)
    ]
    for c in a_copies:
        c.start()

    row_id = lax.broadcasted_iota(I32, (8, 128), 0)
    lane_id = lax.broadcasted_iota(I32, (8, 128), 1)
    tile = jnp.zeros((8, 128), I32)
    for e in range(e_local):
        for lane, value in ((0, cols[0, e]), (1, cols[1, e]), (2, count[e])):
            tile = jnp.where((row_id == e) & (lane_id == lane), value, tile)
    meta[1 + g] = tile

    @pl.when(q == 0)
    def _():
        meta[0] = jnp.zeros((8, 128), I32)
        for i in range(8):
            from_prev[i] = jnp.zeros(from_prev.shape[1:], F32)

    @pl.when(q == n_rows - 1)
    def _():
        meta[5] = jnp.zeros((8, 128), I32)
        for i in range(8):
            from_next[i] = jnp.zeros(from_next.shape[1:], F32)

    barrier = pltpu.get_barrier_semaphore()
    for dev in (yp, ym):
        pl.semaphore_signal(barrier, inc=1, device_id=dev, device_id_type=MESH)

    @pl.when(has_next)
    def _():
        pl.semaphore_signal(barrier, inc=1, device_id=zp, device_id_type=MESH)

    @pl.when(has_prev)
    def _():
        pl.semaphore_signal(barrier, inc=1, device_id=zm, device_id_type=MESH)

    pl.semaphore_wait(barrier, 2 + has_next.astype(I32) + has_prev.astype(I32))

    def place(src_g, e):
        return p_win.at[e_local + e_local * src_g + e]

    def send_yp(i):
        if i < 8:
            src, dst = p_hbm.at[i], place(g, i)
        elif i == 8:
            src = dst = meta.at[1 + g]
        elif i < 13:
            src = dst = place(down, i - 9)
        else:
            src = dst = meta.at[1 + down]
        return copy(src, dst, yp_s.at[i], yp_r.at[i], yp)

    def send_ym(i):
        if i < 8:
            src, dst = p_hbm.at[i], place(g, i)
        elif i == 8:
            src = dst = meta.at[1 + g]
        else:
            src = dst = place(up, half + i - 9)
        return copy(src, dst, ym_s.at[i], ym_r.at[i], ym)

    def send_zp(e):
        if e < 8:
            src, dst = place(3, e), p_win.at[e]
        else:
            src, dst = meta.at[4], meta.at[0]
        return copy(src, dst, zp_s.at[e], zp_r.at[e], zp)

    def send_zm(e):
        if e < 8:
            src, dst = place(0, e), p_win.at[5 * e_local + e]
        else:
            src, dst = meta.at[1], meta.at[5]
        return copy(src, dst, zm_s.at[e], zm_r.at[e], zm)

    def rim(src_g, e):
        @pl.when((src_g == 3) & has_next)
        def _():
            send_zp(e).start()

        @pl.when((src_g == 0) & has_prev)
        def _():
            send_zm(e).start()

    def widen(index):
        for l in range(2):
            high, low = split(p_win[index, l])
            lanes = pl.ds(l * size, size)
            p3[index, pl.ds(0, size), lanes] = high
            p3[index, pl.ds(size, size), lanes] = high
            p3[index, pl.ds(2 * size, size), lanes] = low

    def prepare(e):
        a_copies[e].wait()
        for k in range(n_slot):
            high, low = split(a_f32[e, k])
            a3[e * n_slot + k, :, pl.ds(0, size)] = high
            a3[e * n_slot + k, :, pl.ds(size, size)] = low
            a3[e * n_slot + k, :, pl.ds(2 * size, size)] = high
        for j in range(2):
            high, low = split(p_win[e_local + e_local * g + e, j].T)
            pt3[2 * e + j, :, pl.ds(0, size)] = high
            pt3[2 * e + j, :, pl.ds(size, size)] = low
            pt3[2 * e + j, :, pl.ds(2 * size, size)] = high

    base = q * (4 * e_local) - e_local
    n_block = 2 * n_slot
    meta_copy = pltpu.make_async_copy(meta, meta_s, m_sem.at[0])

    def plan(e, carry):
        columns = []
        live_k = near_count[e]
        for k in range(n_slot):
            n = jnp.clip(near[e, k] - base, 0, 6 * e_local - 1)
            n_s[e * n_slot + k] = n
            n_hi, n_lo = lax.shift_right_logical(n, 3), n & 7
            live_l = jnp.where(k < live_k, meta_s[n_hi, n_lo, 2], 0)
            for l in range(2):
                columns.append(jnp.where(l < live_l, meta_s[n_hi, n_lo, l], -1))
        for x in range(n_block):
            found = n_block
            for y in range(x):
                found = jnp.where(columns[y] == columns[x], y, found)
            prev_s[e * n_block + x] = jnp.int32(found)
        live_j = count[e]
        for j in range(2):
            c = cols[j, e]
            for s in range(4):
                target = jnp.where(j < live_j, pattern[s, c], -2)
                found = n_block
                for x in range(n_block):
                    found = jnp.where(columns[x] == target, x, found)
                last_s[e * 8 + 4 * j + s] = found
        return carry

    send_yp(8).start()
    send_ym(8).start()
    for i in range(half):
        send_yp(i).start()
        send_ym(half + i).start()
    own_copy.wait()
    for sums in (sums_a, sums_b):
        sums[n_block] = jnp.zeros((size, size), F32)
    for e in range(9):
        rim(g, e)
    send_yp(8).wait_recv()
    send_yp(13).start()
    rim(down, 8)
    send_ym(8).wait_recv()
    rim(up, 8)
    for e in range(e_local):
        widen(e_local + e_local * g + e)
    for i in range(half):
        send_yp(i).wait_recv()
        send_yp(9 + i).start()
        send_yp(half + i).start()
        rim(down, i)
        send_ym(half + i).wait_recv()
        send_ym(9 + i).start()
        send_ym(i).start()
        rim(up, half + i)
        if i == 0:
            send_yp(13).wait_recv()
            rim(opp, 8)
        widen(e_local + e_local * down + i)
        widen(e_local + e_local * up + half + i)
        prepare(2 * i)
        prepare(2 * i + 1)
    for i in range(half):
        send_yp(9 + i).wait_recv()
        rim(opp, i)
        send_ym(9 + i).wait_recv()
        rim(opp, half + i)
        send_yp(half + i).wait_recv()
        rim(down, half + i)
        send_ym(i).wait_recv()
        rim(up, i)
        widen(e_local + e_local * opp + i)
        widen(e_local + e_local * opp + half + i)
        widen(e_local + e_local * down + half + i)
        widen(e_local + e_local * up + i)
        if i == 0:
            @pl.when(has_prev)
            def _():
                send_zp(8).wait_recv()

            @pl.when(has_next)
            def _():
                send_zm(8).wait_recv()

            meta_copy.start()
        if i == 1:
            meta_copy.wait()
            lax.fori_loop(0, e_local, plan, 0)

    for e in range(e_local):
        @pl.when(has_prev)
        def _():
            send_zp(e).wait_recv()
            widen(e)

        @pl.when(has_next)
        def _():
            send_zm(e).wait_recv()
            widen(5 * e_local + e)

    def element(e, sums, z3):
        for k in range(n_slot):
            d = jnp.dot(
                a3[e * n_slot + k], p3[n_s[e * n_slot + k]], preferred_element_type=F32
            )
            for l in range(2):
                x = 2 * k + l
                sums[x] = d[:, l * size : (l + 1) * size] + sums[prev_s[e * n_block + x]]
        for j in range(2):
            for s in range(4):
                high, low = split(sums[last_s[e * 8 + 4 * j + s]])
                lanes = pl.ds(s * size, size)
                z3[j, pl.ds(0, size), lanes] = high
                z3[j, pl.ds(size, size), lanes] = high
                z3[j, pl.ds(2 * size, size), lanes] = low
            term = jnp.dot(pt3[2 * e + j], z3[j], preferred_element_type=F32)
            for s in range(4):
                terms[2 * e + j, s] = term[:, s * size : (s + 1) * size]

    def pair(i, carry):
        element(2 * i, sums_a, z_a)
        element(2 * i + 1, sums_b, z_b)
        return carry

    lax.fori_loop(0, e_local // 2, pair, 0)

    where = []
    for e in range(e_local):
        for j in range(2):
            c = cols[j, e]
            where.append((lax.shift_right_logical(c, 2) - q + 1) * 4 + slot[c])

    def gather_rows(dst, i, first, slots):
        rel, h = ORDER[i]
        target = first + lax.rem(g + rel, 4)
        for s in range(2):
            total = None
            for x in slots:
                match = jnp.where(where[x] == target, 1.0, 0.0)
                part = terms[x, 2 * h + s] * match
                total = part if total is None else total + part
            dst[i, s] = total

    def send_tp(i):
        return copy(to_prev.at[i], from_next.at[i], tp_s.at[i], tp_r.at[i], zm)

    def send_tn(i):
        return copy(to_next.at[i], from_prev.at[i], tn_s.at[i], tn_r.at[i], zp)

    seconds = [2 * e + 1 for e in range(e_local)]
    for i in range(8):
        @pl.when(has_prev)
        def _():
            gather_rows(to_prev, i, 0, seconds)
            send_tp(i).start()

        @pl.when(has_next)
        def _():
            gather_rows(to_next, i, 8, seconds)
            send_tn(i).start()

    for i in range(8):
        gather_rows(own, i, 4, range(2 * e_local))

    def send_y(i):
        return copy(
            own.at[i], from_y.at[i], ty_s.at[i], ty_r.at[i], yp if i in (0, 2, 4) else ym
        )

    for i in range(8):
        @pl.when(has_next)
        def _():
            send_tp(i).wait_recv()

        @pl.when(has_prev)
        def _():
            send_tn(i).wait_recv()

        total = own[i] + (from_next[i] + from_prev[i])
        if i in (4, 5):
            send_y(i - 4).wait_recv()
            total = total + from_y[i - 4]
        own[i] = total
        if i < 6:
            send_y(i).start()
    for i in (3, 2, 4, 5):
        send_y(i).wait_recv()
    for s in range(2):
        out[0, s] = own[6, s] + (from_y[4, s] + from_y[3, s])
        out[0, 2 + s] = own[7, s] + (from_y[2, s] + from_y[5, s])

    for i in range(14):
        send_yp(i).wait_send()
    for i in range(13):
        send_ym(i).wait_send()

    @pl.when(has_next)
    def _():
        for e in range(9):
            send_zp(e).wait_send()
        for i in range(8):
            send_tn(i).wait_send()

    @pl.when(has_prev)
    def _():
        for e in range(9):
            send_zm(e).wait_send()
        for i in range(8):
            send_tp(i).wait_send()

    for i in range(6):
        send_y(i).wait_send()


def per_device(a, near, near_count, p, cols, count, slot, pattern):
    e_local, n_slot, size = a.shape[0], a.shape[1], a.shape[2]
    smem = pl.BlockSpec(memory_space=pltpu.SMEM)
    anywhere = pl.BlockSpec(memory_space=pl.ANY)
    dma = pltpu.SemaphoreType.DMA
    block = (size, size)
    return pl.pallas_call(
        functools.partial(kernel, lax.axis_size("rows")),
        out_shape=jax.ShapeDtypeStruct((1, 4) + block, F32),
        in_specs=[anywhere, smem, smem, anywhere, smem, smem, smem, smem],
        out_specs=pl.BlockSpec(memory_space=pltpu.VMEM),
        scratch_shapes=[
            pltpu.VMEM(a.shape, F32),
            pltpu.VMEM((e_local * n_slot, size, 3 * size), BF16),
            pltpu.VMEM((6 * e_local, 2) + block, F32),
            pltpu.VMEM((6 * e_local, 3 * size, 2 * size), BF16),
            pltpu.VMEM((2 * e_local, size, 3 * size), BF16),
            pltpu.VMEM((2 * n_slot + 1,) + block, F32),
            pltpu.VMEM((2 * n_slot + 1,) + block, F32),
            pltpu.VMEM((2, 3 * size, 4 * size), BF16),
            pltpu.VMEM((2, 3 * size, 4 * size), BF16),
            pltpu.VMEM((2 * e_local, 4) + block, F32),
            pltpu.VMEM((6, 8, 128), I32),
            pltpu.SMEM((6, 8, 128), I32),
            pltpu.SMEM((e_local * n_slot,), I32),
            pltpu.SMEM((2 * e_local * n_slot,), I32),
            pltpu.SMEM((8 * e_local,), I32),
        ]
        + [pltpu.VMEM((8, 2) + block, F32)] * 5
        + [pltpu.VMEM((6, 2) + block, F32)]
        + [dma((e_local,)), dma((1,)), dma((1,))]
        + [dma((14,)), dma((14,)), dma((13,)), dma((13,))]
        + [dma((9,))] * 4
        + [dma((8,))] * 4
        + [dma((6,))] * 2,
        compiler_params=pltpu.CompilerParams(
            collective_id=0, has_side_effects=True, vmem_limit_bytes=56 << 20
        ),
    )(a, near, near_count, p, cols.T, count, slot, pattern.T)


def solution(mesh):
    return jax.shard_map(
        per_device,
        mesh=mesh,
        in_specs=(
            P(("rows", "grp"), None, None, None),
            P(("rows", "grp"), None),
            P(("rows", "grp")),
            P(("rows", "grp"), None, None, None),
            P(("rows", "grp"), None),
            P(("rows", "grp")),
            P(),
            P(),
        ),
        out_specs=P(("rows", "grp"), None, None, None),
        check_vma=False,
    )
```

```python
import functools

import jax
import jax.numpy as jnp
from jax import lax
from jax.experimental import pallas as pl
from jax.experimental.pallas import tpu as pltpu
from jax.sharding import PartitionSpec as P

MESH = pl.DeviceIdType.MESH
F32, BF16, I32 = jnp.float32, jnp.bfloat16, jnp.int32
ORDER = (
    (2, 0), (2, 2), (2, 1), (2, 3), (1, 2), (3, 0), (1, 3), (3, 1),
    (1, 0), (3, 2), (1, 1), (3, 3), (0, 0), (0, 1), (0, 2), (0, 3),
)


def split(value):
    high = value.astype(BF16)
    return high, (value - high.astype(F32)).astype(BF16)


def kernel(
    n_rows, a_hbm, near_hbm, near_count_hbm, p_hbm, cols_hbm, count_hbm, slot_hbm, pattern_hbm, out,
    near, near_count, cols, count, slot, pattern,
    a_f32, a3, p_win, p3, pt3, sums_a, sums_b, z_a, z_b, z_first, terms, meta, meta_s,
    n_s, prev_s, last_s,
    to_prev, to_next, from_next, from_prev, own, from_y,
    a_sem, p_sem, m_sem, i_sem,
    yp_s, yp_r, ym_s, ym_r, zp_s, zp_r, zm_s, zm_r,
    tn_s, tn_r, tp_s, tp_r, ty_s, ty_r,
):
    e_local, n_slot, size = a_hbm.shape[0], a_hbm.shape[1], a_hbm.shape[2]
    half = e_local // 2
    q, g = lax.axis_index("rows"), lax.axis_index("grp")
    up, down, opp = lax.rem(g + 1, 4), lax.rem(g + 3, 4), lax.rem(g + 2, 4)
    has_prev, has_next = q > 0, q < n_rows - 1
    yp, ym = {"grp": up}, {"grp": down}
    zp, zm = {"rows": q + 1}, {"rows": q - 1}

    def copy(src, dst, ssem, rsem, dev):
        return pltpu.make_async_remote_copy(
            src_ref=src, dst_ref=dst, send_sem=ssem, recv_sem=rsem,
            device_id=dev, device_id_type=MESH,
        )

    barrier = pltpu.get_barrier_semaphore()
    for dev in (yp, ym):
        pl.semaphore_signal(barrier, inc=1, device_id=dev, device_id_type=MESH)

    @pl.when(has_next)
    def _():
        pl.semaphore_signal(barrier, inc=1, device_id=zp, device_id_type=MESH)

    @pl.when(has_prev)
    def _():
        pl.semaphore_signal(barrier, inc=1, device_id=zm, device_id_type=MESH)

    index_copies = [
        pltpu.make_async_copy(src, dst, i_sem.at[i])
        for i, (src, dst) in enumerate((
            (cols_hbm, cols), (count_hbm, count), (near_hbm, near),
            (near_count_hbm, near_count), (slot_hbm, slot), (pattern_hbm, pattern),
        ))
    ]
    for c in index_copies:
        c.start()
    own_copy = pltpu.make_async_copy(
        p_hbm, p_win.at[pl.ds(e_local + e_local * g, e_local)], p_sem.at[0]
    )
    own_copy.start()

    @pl.when(q == 0)
    def _():
        meta[0] = jnp.zeros((8, 128), I32)
        for i in range(16):
            from_prev[i] = jnp.zeros(from_prev.shape[1:], F32)

    @pl.when(q == n_rows - 1)
    def _():
        meta[5] = jnp.zeros((8, 128), I32)
        for i in range(16):
            from_next[i] = jnp.zeros(from_next.shape[1:], F32)

    for c in index_copies:
        c.wait()
    row_id = lax.broadcasted_iota(I32, (8, 128), 0)
    lane_id = lax.broadcasted_iota(I32, (8, 128), 1)
    tile = jnp.zeros((8, 128), I32)
    for e in range(e_local):
        for lane, value in ((0, cols[0, e]), (1, cols[1, e]), (2, count[e])):
            tile = jnp.where((row_id == e) & (lane_id == lane), value, tile)
    meta[1 + g] = tile

    pl.semaphore_wait(barrier, 2 + has_next.astype(I32) + has_prev.astype(I32))

    a_copies = [
        pltpu.make_async_copy(a_hbm.at[e], a_f32.at[e], a_sem.at[e])
        for e in range(e_local)
    ]

    def place(src_g, e):
        return p_win.at[e_local + e_local * src_g + e]

    def send_yp(i):
        if i < 8:
            src, dst = p_hbm.at[i], place(g, i)
        elif i == 8:
            src = dst = meta.at[1 + g]
        elif i < 13:
            src = dst = place(down, i - 9)
        else:
            src = dst = meta.at[1 + down]
        return copy(src, dst, yp_s.at[i], yp_r.at[i], yp)

    def send_ym(i):
        if i < 8:
            src, dst = p_hbm.at[i], place(g, i)
        elif i == 8:
            src = dst = meta.at[1 + g]
        else:
            src = dst = place(up, half + i - 9)
        return copy(src, dst, ym_s.at[i], ym_r.at[i], ym)

    def send_zp(e, mine=False):
        if e < 8:
            src, dst = (p_hbm.at[e] if mine else place(3, e)), p_win.at[e]
        else:
            src, dst = meta.at[4], meta.at[0]
        return copy(src, dst, zp_s.at[e], zp_r.at[e], zp)

    def send_zm(e, mine=False):
        if e < 8:
            src, dst = (p_hbm.at[e] if mine else place(0, e)), p_win.at[5 * e_local + e]
        else:
            src, dst = meta.at[1], meta.at[5]
        return copy(src, dst, zm_s.at[e], zm_r.at[e], zm)

    def rim(src_g, e):
        mine = src_g is g
        @pl.when((src_g == 3) & has_next)
        def _():
            send_zp(e, mine).start()

        @pl.when((src_g == 0) & has_prev)
        def _():
            send_zm(e, mine).start()

    def widen(index):
        for l in range(2):
            high, low = split(p_win[index, l])
            lanes = pl.ds(l * size, size)
            p3[index, pl.ds(0, size), lanes] = high
            p3[index, pl.ds(size, size), lanes] = high
            p3[index, pl.ds(2 * size, size), lanes] = low

    def prepare(e):
        a_copies[e].wait()
        for k in range(n_slot):
            high, low = split(a_f32[e, k])
            a3[e * n_slot + k, :, pl.ds(0, size)] = high
            a3[e * n_slot + k, :, pl.ds(size, size)] = low
            a3[e * n_slot + k, :, pl.ds(2 * size, size)] = high
        for j in range(2):
            high, low = split(p_win[e_local + e_local * g + e, j].T)
            pt3[2 * e + j, :, pl.ds(0, size)] = high
            pt3[2 * e + j, :, pl.ds(size, size)] = low
            pt3[2 * e + j, :, pl.ds(2 * size, size)] = high

    base = q * (4 * e_local) - e_local
    n_block = 2 * n_slot
    meta_copy = pltpu.make_async_copy(meta, meta_s, m_sem.at[0])

    def plan(e, carry):
        columns = []
        live_k = near_count[e]
        for k in range(n_slot):
            n = jnp.clip(near[e, k] - base, 0, 6 * e_local - 1)
            n_s[e * n_slot + k] = n
            n_hi, n_lo = lax.shift_right_logical(n, 3), n & 7
            live_l = jnp.where(k < live_k, meta_s[n_hi, n_lo, 2], 0)
            for l in range(2):
                columns.append(jnp.where(l < live_l, meta_s[n_hi, n_lo, l], -1))
        for x in range(n_block):
            found = n_block
            for y in range(x):
                found = jnp.where(columns[y] == columns[x], y, found)
            prev_s[e * n_block + x] = jnp.int32(found)
        live_j = count[e]
        for j in range(2):
            c = cols[j, e]
            for s in range(4):
                target = jnp.where(j < live_j, pattern[s, c], -2)
                found = n_block
                for x in range(n_block):
                    found = jnp.where(columns[x] == target, x, found)
                last_s[e * 8 + 4 * j + s] = found
        return carry

    send_yp(8).start()
    send_ym(8).start()
    for i in range(half):
        send_yp(i).start()
        send_ym(half + i).start()
    for e in (8, *range(8)):
        rim(g, e)
    for c in a_copies:
        c.start()

    for sums in (sums_a, sums_b):
        sums[n_block] = jnp.zeros((size, size), F32)
    own_copy.wait()
    for e in range(e_local):
        widen(e_local + e_local * g + e)
    send_yp(8).wait_recv()
    send_yp(13).start()
    rim(down, 8)
    send_ym(8).wait_recv()
    rim(up, 8)
    edge = lax.rem(q, 2) * 3
    own_first, down_first, up_first = g == edge, down == edge, up == edge

    def pieces(relayed, mine):
        @pl.when(own_first)
        def _():
            mine.start()
            relayed.start()

        @pl.when(jnp.logical_not(own_first))
        def _():
            relayed.start()
            mine.start()

    for i in range(half):
        send_yp(i).wait_recv()
        pieces(send_yp(9 + i), send_yp(half + i))
        rim(down, i)
        send_ym(half + i).wait_recv()
        pieces(send_ym(9 + i), send_ym(i))
        rim(up, half + i)
        if i == 0:
            send_yp(13).wait_recv()
            rim(opp, 8)
        widen(e_local + e_local * down + i)
        widen(e_local + e_local * up + half + i)
        prepare(2 * i)
        prepare(2 * i + 1)
    for i in range(half):
        def from_down():
            send_yp(half + i).wait_recv()
            rim(down, half + i)

        def from_up():
            send_ym(i).wait_recv()
            rim(up, i)

        pl.when(down_first)(from_down)
        pl.when(up_first)(from_up)
        send_yp(9 + i).wait_recv()
        rim(opp, i)
        send_ym(9 + i).wait_recv()
        rim(opp, half + i)
        pl.when(jnp.logical_not(down_first))(from_down)
        pl.when(jnp.logical_not(up_first))(from_up)
        widen(e_local + e_local * opp + i)
        widen(e_local + e_local * opp + half + i)
        widen(e_local + e_local * down + half + i)
        widen(e_local + e_local * up + i)
        if i == 0:
            @pl.when(has_prev)
            def _():
                send_zp(8).wait_recv()

            @pl.when(has_next)
            def _():
                send_zm(8).wait_recv()

            meta_copy.start()
        if i == 1:
            meta_copy.wait()
            lax.fori_loop(0, e_local, plan, 0)

    for e in range(e_local):
        @pl.when(has_prev)
        def _():
            send_zp(e).wait_recv()
            widen(e)

        @pl.when(has_next)
        def _():
            send_zm(e).wait_recv()
            widen(5 * e_local + e)

    def element(e, sums, z3):
        for k in range(n_slot):
            d = jnp.dot(
                a3[e * n_slot + k], p3[n_s[e * n_slot + k]], preferred_element_type=F32
            )
            for l in range(2):
                x = 2 * k + l
                sums[x] = d[:, l * size : (l + 1) * size] + sums[prev_s[e * n_block + x]]
        for j in range(2):
            dst = z3 if j else z_first.at[e]
            for s in range(4):
                high, low = split(sums[last_s[e * 8 + 4 * j + s]])
                lanes = pl.ds(s * size, size)
                dst[pl.ds(0, size), lanes] = high
                dst[pl.ds(size, size), lanes] = high
                dst[pl.ds(2 * size, size), lanes] = low
        finish(2 * e + 1, z3[...])

    def finish(x, z):
        term = jnp.dot(pt3[x], z, preferred_element_type=F32)
        for s in range(4):
            terms[x, s] = term[:, s * size : (s + 1) * size]

    def pair(i, carry):
        element(2 * i, sums_a, z_a)
        element(2 * i + 1, sums_b, z_b)
        return carry

    lax.fori_loop(0, e_local // 2, pair, 0)

    where = []
    for e in range(e_local):
        for j in range(2):
            c = cols[j, e]
            where.append((lax.shift_right_logical(c, 2) - q + 1) * 4 + slot[c])

    def gather_rows(dst, i, first, slots):
        rel, s = ORDER[i]
        target = first + lax.rem(g + rel, 4)
        total = None
        for x in slots:
            match = jnp.where(where[x] == target, 1.0, 0.0)
            part = terms[x, s] * match
            total = part if total is None else total + part
        dst[i] = total

    def send_tp(i):
        return copy(to_prev.at[i], from_next.at[i], tp_s.at[i], tp_r.at[i], zm)

    def send_tn(i):
        return copy(to_next.at[i], from_prev.at[i], tn_s.at[i], tn_r.at[i], zp)

    seconds = [2 * e + 1 for e in range(e_local)]
    for i in range(16):
        @pl.when(has_prev)
        def _():
            gather_rows(to_prev, i, 0, seconds)
            send_tp(i).start()

        @pl.when(has_next)
        def _():
            gather_rows(to_next, i, 8, seconds)
            send_tn(i).start()

    def first_slot(e, carry):
        finish(2 * e, z_first[e])
        return carry

    lax.fori_loop(0, e_local, first_slot, 0)

    def send_y(i):
        return copy(
            own.at[i], from_y.at[i], ty_s.at[i], ty_r.at[i], ym if i % 2 else yp
        )

    for i in range(16):
        gather_rows(own, i, 4, range(2 * e_local))

        @pl.when(has_next)
        def _():
            send_tp(i).wait_recv()

        @pl.when(has_prev)
        def _():
            send_tn(i).wait_recv()

        total = own[i] + (from_next[i] + from_prev[i])
        if 8 <= i < 12:
            send_y(i - 8).wait_recv()
            total = total + from_y[i - 8]
        own[i] = total
        if i < 12:
            send_y(i).start()
    for i in range(4, 12):
        send_y(i).wait_recv()
    for s, parts in enumerate(((8, 5), (10, 7), (4, 9), (6, 11))):
        out[0, s] = own[12 + s] + (from_y[parts[0]] + from_y[parts[1]])

    for i in range(14):
        send_yp(i).wait_send()
    for i in range(13):
        send_ym(i).wait_send()

    @pl.when(has_next)
    def _():
        for e in range(9):
            send_zp(e).wait_send()
        for i in range(16):
            send_tn(i).wait_send()

    @pl.when(has_prev)
    def _():
        for e in range(9):
            send_zm(e).wait_send()
        for i in range(16):
            send_tp(i).wait_send()

    for i in range(12):
        send_y(i).wait_send()


def per_device(a, near, near_count, p, cols, count, slot, pattern):
    e_local, n_slot, size = a.shape[0], a.shape[1], a.shape[2]
    anywhere = pl.BlockSpec(memory_space=pl.ANY)
    dma = pltpu.SemaphoreType.DMA
    block = (size, size)
    return pl.pallas_call(
        functools.partial(kernel, lax.axis_size("rows")),
        out_shape=pltpu.VMEM((1, 4) + block, F32),
        in_specs=[anywhere] * 8,
        out_specs=pl.BlockSpec(memory_space=pltpu.VMEM),
        scratch_shapes=[
            pltpu.SMEM(x.shape, I32)
            for x in (near, near_count, cols.T, count, slot, pattern.T)
        ]
        + [
            pltpu.VMEM(a.shape, F32),
            pltpu.VMEM((e_local * n_slot, size, 3 * size), BF16),
            pltpu.VMEM((6 * e_local, 2) + block, F32),
            pltpu.VMEM((6 * e_local, 3 * size, 2 * size), BF16),
            pltpu.VMEM((2 * e_local, size, 3 * size), BF16),
            pltpu.VMEM((2 * n_slot + 1,) + block, F32),
            pltpu.VMEM((2 * n_slot + 1,) + block, F32),
            pltpu.VMEM((3 * size, 4 * size), BF16),
            pltpu.VMEM((3 * size, 4 * size), BF16),
            pltpu.VMEM((e_local, 3 * size, 4 * size), BF16),
            pltpu.VMEM((2 * e_local, 4) + block, F32),
            pltpu.VMEM((6, 8, 128), I32),
            pltpu.SMEM((6, 8, 128), I32),
            pltpu.SMEM((e_local * n_slot,), I32),
            pltpu.SMEM((2 * e_local * n_slot,), I32),
            pltpu.SMEM((8 * e_local,), I32),
        ]
        + [pltpu.VMEM((16,) + block, F32)] * 5
        + [pltpu.VMEM((12,) + block, F32)]
        + [dma((e_local,)), dma((1,)), dma((1,)), dma((6,))]
        + [dma((14,)), dma((14,)), dma((13,)), dma((13,))]
        + [dma((9,))] * 4
        + [dma((16,))] * 4
        + [dma((12,))] * 2,
        compiler_params=pltpu.CompilerParams(
            collective_id=0, has_side_effects=True, vmem_limit_bytes=56 << 20
        ),
    )(a, near, near_count, p, cols.T, count, slot, pattern.T)


def solution(mesh):
    return jax.shard_map(
        per_device,
        mesh=mesh,
        in_specs=(
            P(("rows", "grp"), None, None, None),
            P(("rows", "grp"), None),
            P(("rows", "grp")),
            P(("rows", "grp"), None, None, None),
            P(("rows", "grp"), None),
            P(("rows", "grp")),
            P(),
            P(),
        ),
        out_specs=P(("rows", "grp"), None, None, None),
        check_vma=False,
    )
```

```python
import functools

import jax
import jax.numpy as jnp
from jax import lax
from jax.experimental import pallas as pl
from jax.experimental.pallas import tpu as pltpu
from jax.sharding import PartitionSpec as P

MESH = pl.DeviceIdType.MESH
F32, BF16, I32 = jnp.float32, jnp.bfloat16, jnp.int32
ORDER = (
    (2, 0), (2, 2), (2, 1), (2, 3), (1, 2), (3, 0), (1, 3), (3, 1),
    (1, 0), (3, 2), (1, 1), (3, 3), (0, 0), (0, 1), (0, 2), (0, 3),
)


def split(value):
    high = value.astype(BF16)
    return high, (value - high.astype(F32)).astype(BF16)


def kernel(
    n_rows, a_hbm, near_hbm, near_count_hbm, p_hbm, cols_hbm, count_hbm, slot_hbm, pattern_hbm, out,
    near, near_count, cols, count, slot, pattern,
    a_f32, a3, p_win, p3, pt3, sums_a, sums_b, z_a, z_b, z_first, terms, meta, meta_s,
    n_s, prev_s, last_s, first,
    to_prev, to_next, from_next, from_prev, own, from_y,
    a_sem, p_sem, m_sem, i_sem,
    yp_s, yp_r, ym_s, ym_r, zp_s, zp_r, zm_s, zm_r,
    tn_s, tn_r, tp_s, tp_r, ty_s, ty_r,
):
    e_local, n_slot, size = a_hbm.shape[0], a_hbm.shape[1], a_hbm.shape[2]
    half = e_local // 2
    q, g = lax.axis_index("rows"), lax.axis_index("grp")
    up, down, opp = lax.rem(g + 1, 4), lax.rem(g + 3, 4), lax.rem(g + 2, 4)
    has_prev, has_next = q > 0, q < n_rows - 1
    yp, ym = {"grp": up}, {"grp": down}
    zp, zm = {"rows": q + 1}, {"rows": q - 1}

    def copy(src, dst, ssem, rsem, dev):
        return pltpu.make_async_remote_copy(
            src_ref=src, dst_ref=dst, send_sem=ssem, recv_sem=rsem,
            device_id=dev, device_id_type=MESH,
        )

    barrier = pltpu.get_barrier_semaphore()
    for dev in (yp, ym):
        pl.semaphore_signal(barrier, inc=1, device_id=dev, device_id_type=MESH)

    @pl.when(has_next)
    def _():
        pl.semaphore_signal(barrier, inc=1, device_id=zp, device_id_type=MESH)

    @pl.when(has_prev)
    def _():
        pl.semaphore_signal(barrier, inc=1, device_id=zm, device_id_type=MESH)

    index_copies = [
        pltpu.make_async_copy(src, dst, i_sem.at[i])
        for i, (src, dst) in enumerate((
            (cols_hbm, cols), (count_hbm, count), (near_hbm, near),
            (near_count_hbm, near_count), (slot_hbm, slot), (pattern_hbm, pattern),
        ))
    ]
    for c in index_copies:
        c.start()
    own_copy = pltpu.make_async_copy(
        p_hbm, p_win.at[pl.ds(e_local + e_local * g, e_local)], p_sem.at[0]
    )
    own_copy.start()

    @pl.when(q == 0)
    def _():
        meta[0] = jnp.zeros((8, 128), I32)
        for i in range(16):
            from_prev[i] = jnp.zeros(from_prev.shape[1:], F32)

    @pl.when(q == n_rows - 1)
    def _():
        meta[5] = jnp.zeros((8, 128), I32)
        for i in range(16):
            from_next[i] = jnp.zeros(from_next.shape[1:], F32)

    for c in index_copies:
        c.wait()
    row_id = lax.broadcasted_iota(I32, (8, 128), 0)
    lane_id = lax.broadcasted_iota(I32, (8, 128), 1)
    tile = jnp.zeros((8, 128), I32)
    for e in range(e_local):
        for lane, value in ((0, cols[0, e]), (1, cols[1, e]), (2, count[e])):
            tile = jnp.where((row_id == e) & (lane_id == lane), value, tile)
    meta[1 + g] = tile

    pl.semaphore_wait(barrier, 2 + has_next.astype(I32) + has_prev.astype(I32))

    a_copies = [
        pltpu.make_async_copy(a_hbm.at[e], a_f32.at[e], a_sem.at[e])
        for e in range(e_local)
    ]

    def place(src_g, e):
        return p_win.at[e_local + e_local * src_g + e]

    def send_yp(i):
        if i < 8:
            src, dst = p_hbm.at[i], place(g, i)
        elif i == 8:
            src = dst = meta.at[1 + g]
        elif i < 13:
            src = dst = place(down, i - 9)
        else:
            src = dst = meta.at[1 + down]
        return copy(src, dst, yp_s.at[i], yp_r.at[i], yp)

    def send_ym(i):
        if i < 8:
            src, dst = p_hbm.at[i], place(g, i)
        elif i == 8:
            src = dst = meta.at[1 + g]
        else:
            src = dst = place(up, half + i - 9)
        return copy(src, dst, ym_s.at[i], ym_r.at[i], ym)

    def send_zp(e, mine=False):
        if e < 8:
            src, dst = (p_hbm.at[e] if mine else place(3, e)), p_win.at[e]
        else:
            src, dst = meta.at[4], meta.at[0]
        return copy(src, dst, zp_s.at[e], zp_r.at[e], zp)

    def send_zm(e, mine=False):
        if e < 8:
            src, dst = (p_hbm.at[e] if mine else place(0, e)), p_win.at[5 * e_local + e]
        else:
            src, dst = meta.at[1], meta.at[5]
        return copy(src, dst, zm_s.at[e], zm_r.at[e], zm)

    def rim(src_g, e):
        mine = src_g is g
        @pl.when((src_g == 3) & has_next)
        def _():
            send_zp(e, mine).start()

        @pl.when((src_g == 0) & has_prev)
        def _():
            send_zm(e, mine).start()

    def widen(index):
        for l in range(2):
            high, low = split(p_win[index, l])
            lanes = pl.ds(l * size, size)
            p3[index, pl.ds(0, size), lanes] = high
            p3[index, pl.ds(size, size), lanes] = high
            p3[index, pl.ds(2 * size, size), lanes] = low

    def prepare(e):
        a_copies[e].wait()
        for k in range(n_slot):
            high, low = split(a_f32[e, k])
            a3[e * n_slot + k, :, pl.ds(0, size)] = high
            a3[e * n_slot + k, :, pl.ds(size, size)] = low
            a3[e * n_slot + k, :, pl.ds(2 * size, size)] = high
        first[e] = jnp.dot(
            a3[e * n_slot], p3[e_local + e_local * g + e], preferred_element_type=F32
        )
        for j in range(2):
            high, low = split(p_win[e_local + e_local * g + e, j].T)
            pt3[2 * e + j, :, pl.ds(0, size)] = high
            pt3[2 * e + j, :, pl.ds(size, size)] = low
            pt3[2 * e + j, :, pl.ds(2 * size, size)] = high

    base = q * (4 * e_local) - e_local
    n_block = 2 * n_slot
    meta_copy = pltpu.make_async_copy(meta, meta_s, m_sem.at[0])

    def plan(e, carry):
        columns = []
        live_k = near_count[e]
        for k in range(n_slot):
            n = jnp.clip(near[e, k] - base, 0, 6 * e_local - 1)
            n_s[e * n_slot + k] = n
            n_hi, n_lo = lax.shift_right_logical(n, 3), n & 7
            live_l = jnp.where(k < live_k, meta_s[n_hi, n_lo, 2], 0)
            for l in range(2):
                columns.append(jnp.where(l < live_l, meta_s[n_hi, n_lo, l], -1))
        for x in range(n_block):
            found = n_block
            for y in range(x):
                found = jnp.where(columns[y] == columns[x], y, found)
            prev_s[e * n_block + x] = jnp.int32(found)
        live_j = count[e]
        for j in range(2):
            c = cols[j, e]
            for s in range(4):
                target = jnp.where(j < live_j, pattern[s, c], -2)
                found = n_block
                for x in range(n_block):
                    found = jnp.where(columns[x] == target, x, found)
                last_s[e * 8 + 4 * j + s] = found
        return carry

    send_yp(8).start()
    send_ym(8).start()
    for i in range(half):
        send_yp(i).start()
        send_ym(half + i).start()
    for e in (8, *range(8)):
        rim(g, e)
    for c in a_copies:
        c.start()

    for sums in (sums_a, sums_b):
        sums[n_block] = jnp.zeros((size, size), F32)
    own_copy.wait()
    for e in range(e_local):
        widen(e_local + e_local * g + e)
    send_yp(8).wait_recv()
    send_yp(13).start()
    rim(down, 8)
    send_ym(8).wait_recv()
    rim(up, 8)
    edge = lax.rem(q, 2) * 3
    own_first, down_first, up_first = g == edge, down == edge, up == edge

    def pieces(relayed, mine):
        @pl.when(own_first)
        def _():
            mine.start()
            relayed.start()

        @pl.when(jnp.logical_not(own_first))
        def _():
            relayed.start()
            mine.start()

    for i in range(half):
        send_yp(i).wait_recv()
        pieces(send_yp(9 + i), send_yp(half + i))
        rim(down, i)
        send_ym(half + i).wait_recv()
        pieces(send_ym(9 + i), send_ym(i))
        rim(up, half + i)
        if i == 0:
            send_yp(13).wait_recv()
            rim(opp, 8)
        widen(e_local + e_local * down + i)
        widen(e_local + e_local * up + half + i)
        prepare(2 * i)
        prepare(2 * i + 1)
    for i in range(half):
        def from_down():
            send_yp(half + i).wait_recv()
            rim(down, half + i)

        def from_up():
            send_ym(i).wait_recv()
            rim(up, i)

        pl.when(down_first)(from_down)
        pl.when(up_first)(from_up)
        send_yp(9 + i).wait_recv()
        rim(opp, i)
        send_ym(9 + i).wait_recv()
        rim(opp, half + i)
        pl.when(jnp.logical_not(down_first))(from_down)
        pl.when(jnp.logical_not(up_first))(from_up)
        widen(e_local + e_local * opp + i)
        widen(e_local + e_local * opp + half + i)
        widen(e_local + e_local * down + half + i)
        widen(e_local + e_local * up + i)
        if i == 0:
            @pl.when(has_prev)
            def _():
                send_zp(8).wait_recv()

            @pl.when(has_next)
            def _():
                send_zm(8).wait_recv()

            meta_copy.start()
        if i == 1:
            meta_copy.wait()
            lax.fori_loop(0, e_local, plan, 0)

    for e in range(e_local):
        @pl.when(has_prev)
        def _():
            send_zp(e).wait_recv()
            widen(e)

        @pl.when(has_next)
        def _():
            send_zm(e).wait_recv()
            widen(5 * e_local + e)

    def element(e, sums, z3):
        for k in range(n_slot):
            d = first[e] if k == 0 else jnp.dot(
                a3[e * n_slot + k], p3[n_s[e * n_slot + k]], preferred_element_type=F32
            )
            for l in range(2):
                x = 2 * k + l
                sums[x] = d[:, l * size : (l + 1) * size] + sums[prev_s[e * n_block + x]]
        for j in range(2):
            dst = z3 if j else z_first.at[e]
            for s in range(4):
                high, low = split(sums[last_s[e * 8 + 4 * j + s]])
                lanes = pl.ds(s * size, size)
                dst[pl.ds(0, size), lanes] = high
                dst[pl.ds(size, size), lanes] = high
                dst[pl.ds(2 * size, size), lanes] = low
        finish(2 * e + 1, z3[...])

    def finish(x, z):
        term = jnp.dot(pt3[x], z, preferred_element_type=F32)
        for s in range(4):
            terms[x, s] = term[:, s * size : (s + 1) * size]

    def pair(i, carry):
        element(2 * i, sums_a, z_a)
        element(2 * i + 1, sums_b, z_b)
        return carry

    lax.fori_loop(0, e_local // 2, pair, 0)

    where = []
    for e in range(e_local):
        for j in range(2):
            c = cols[j, e]
            where.append((lax.shift_right_logical(c, 2) - q + 1) * 4 + slot[c])

    def gather_rows(dst, i, first, slots):
        rel, s = ORDER[i]
        target = first + lax.rem(g + rel, 4)
        total = None
        for x in slots:
            match = jnp.where(where[x] == target, 1.0, 0.0)
            part = terms[x, s] * match
            total = part if total is None else total + part
        dst[i] = total

    def send_tp(i):
        return copy(to_prev.at[i], from_next.at[i], tp_s.at[i], tp_r.at[i], zm)

    def send_tn(i):
        return copy(to_next.at[i], from_prev.at[i], tn_s.at[i], tn_r.at[i], zp)

    seconds = [2 * e + 1 for e in range(e_local)]
    for i in range(16):
        @pl.when(has_prev)
        def _():
            gather_rows(to_prev, i, 0, seconds)
            send_tp(i).start()

        @pl.when(has_next)
        def _():
            gather_rows(to_next, i, 8, seconds)
            send_tn(i).start()

    def first_slot(e, carry):
        finish(2 * e, z_first[e])
        return carry

    lax.fori_loop(0, e_local, first_slot, 0)

    def send_y(i):
        return copy(
            own.at[i], from_y.at[i], ty_s.at[i], ty_r.at[i], ym if i % 2 else yp
        )

    for i in range(16):
        gather_rows(own, i, 4, range(2 * e_local))

        @pl.when(has_next)
        def _():
            send_tp(i).wait_recv()

        @pl.when(has_prev)
        def _():
            send_tn(i).wait_recv()

        total = own[i] + (from_next[i] + from_prev[i])
        if 8 <= i < 12:
            send_y(i - 8).wait_recv()
            total = total + from_y[i - 8]
        own[i] = total
        if i < 12:
            send_y(i).start()
    for i in range(4, 12):
        send_y(i).wait_recv()
    for s, parts in enumerate(((8, 5), (10, 7), (4, 9), (6, 11))):
        out[0, s] = own[12 + s] + (from_y[parts[0]] + from_y[parts[1]])

    for i in range(14):
        send_yp(i).wait_send()
    for i in range(13):
        send_ym(i).wait_send()

    @pl.when(has_next)
    def _():
        for e in range(9):
            send_zp(e).wait_send()
        for i in range(16):
            send_tn(i).wait_send()

    @pl.when(has_prev)
    def _():
        for e in range(9):
            send_zm(e).wait_send()
        for i in range(16):
            send_tp(i).wait_send()

    for i in range(12):
        send_y(i).wait_send()


def per_device(a, near, near_count, p, cols, count, slot, pattern):
    e_local, n_slot, size = a.shape[0], a.shape[1], a.shape[2]
    anywhere = pl.BlockSpec(memory_space=pl.ANY)
    dma = pltpu.SemaphoreType.DMA
    block = (size, size)
    return pl.pallas_call(
        functools.partial(kernel, lax.axis_size("rows")),
        out_shape=pltpu.VMEM((1, 4) + block, F32),
        in_specs=[anywhere] * 8,
        out_specs=pl.BlockSpec(memory_space=pltpu.VMEM),
        scratch_shapes=[
            pltpu.SMEM(x.shape, I32)
            for x in (near, near_count, cols.T, count, slot, pattern.T)
        ]
        + [
            pltpu.VMEM(a.shape, F32),
            pltpu.VMEM((e_local * n_slot, size, 3 * size), BF16),
            pltpu.VMEM((6 * e_local, 2) + block, F32),
            pltpu.VMEM((6 * e_local, 3 * size, 2 * size), BF16),
            pltpu.VMEM((2 * e_local, size, 3 * size), BF16),
            pltpu.VMEM((2 * n_slot + 1,) + block, F32),
            pltpu.VMEM((2 * n_slot + 1,) + block, F32),
            pltpu.VMEM((3 * size, 4 * size), BF16),
            pltpu.VMEM((3 * size, 4 * size), BF16),
            pltpu.VMEM((e_local, 3 * size, 4 * size), BF16),
            pltpu.VMEM((2 * e_local, 4) + block, F32),
            pltpu.VMEM((6, 8, 128), I32),
            pltpu.SMEM((6, 8, 128), I32),
            pltpu.SMEM((e_local * n_slot,), I32),
            pltpu.SMEM((2 * e_local * n_slot,), I32),
            pltpu.SMEM((8 * e_local,), I32),
            pltpu.VMEM((e_local, size, 2 * size), F32),
        ]
        + [pltpu.VMEM((16,) + block, F32)] * 5
        + [pltpu.VMEM((12,) + block, F32)]
        + [dma((e_local,)), dma((1,)), dma((1,)), dma((6,))]
        + [dma((14,)), dma((14,)), dma((13,)), dma((13,))]
        + [dma((9,))] * 4
        + [dma((16,))] * 4
        + [dma((12,))] * 2,
        compiler_params=pltpu.CompilerParams(
            collective_id=0, has_side_effects=True, vmem_limit_bytes=56 << 20
        ),
    )(a, near, near_count, p, cols.T, count, slot, pattern.T)


def solution(mesh):
    return jax.shard_map(
        per_device,
        mesh=mesh,
        in_specs=(
            P(("rows", "grp"), None, None, None),
            P(("rows", "grp"), None),
            P(("rows", "grp")),
            P(("rows", "grp"), None, None, None),
            P(("rows", "grp"), None),
            P(("rows", "grp")),
            P(),
            P(),
        ),
        out_specs=P(("rows", "grp"), None, None, None),
        check_vma=False,
    )
```
